32 devices in a mesh: groups: 2 (over x), pb: 16 (over z, y, core).
Axes of the slice: x: 2, y: 2, z: 4, core: 2. Of those that a mesh axis runs over, the one named last changes fastest.
Arguments:
- eigvec: bfloat16 [8192, 2592], P(('groups', 'pb')), parts along dimension 0, may hold values from -0.69921875 to 0.69921875
- omega: bfloat16 [8192, 36], P(('groups', 'pb')), parts along dimension 0, may hold values from 0.5 to 4
- phi: bfloat16 [36, 36, 36], replicated, may hold values from -6 to 6
- send_rows: int32 [32, 32], P(('groups', 'pb')), parts along dimension 0, may hold values from 0 to 255
- local_q: int32 [512], P(('groups', 'pb')), parts along dimension 0, may hold values from 0 to 255
- partner_q: int32 [512], P(('groups', 'pb')), parts along dimension 0, may hold values from 0 to 255
- slot_ref: int32 [512], P(('groups', 'pb')), parts along dimension 0, may hold values from 0 to 31, as said below
- tri_count: int32 [32], P(('groups', 'pb')), parts along dimension 0, may hold values from 8 to 16, as said below
Outputs:
- rates: float32 [36, 8192], P(None, ('groups', 'pb')), parts along dimension 1
The draws below stay inside these ranges and needn't reach their ends.
There are 2 independent parts, one for each index of `groups`. The reference program is written for one: setup_inputs(seed, part) draws one part's arguments, and reference() takes and returns one part's arrays. A program takes and returns all parts, laid end to end along the dimension named above; an argument that names none is the same for every part. Nothing has to cross between parts.
Inputs may be any that keep to these rules, and one draw needn't show every extreme that they name: slot_ref of a live triplet of device p names an owner o and a slot s below the number of slots that o fills for p, which is 1 to 2; each device receives 2 filled slots from some owner. `tri_count`: exactly one device has 16 live triplets; live triplets come first.
All inputs are finite; a program needn't handle non-finite values.
Results may differ from the reference program's by a relative error of at most 0.00048.
Values may be sent and summed in bfloat16 or wider, within the bound.
A program may use at most 128 MiB of HBM per device.

```python
import jax
import jax.numpy as jnp
from jax import lax

NB = 36
QDEV = 256
CAP = 2
TRI_CAP = 16
Q = 4096
TRIPLETS = 256
N_PB = 16


def draw_omega(key, part):
    freq_key = jax.random.fold_in(key, 31)
    logs = jax.random.uniform(freq_key, (QDEV * N_PB, NB), jnp.float32, jnp.log(0.5), jnp.log(4.0))
    values = jnp.clip(jnp.exp(logs), 0.5, 4.0)
    return values.astype(jnp.bfloat16)


def draw_slot_ref(key, part):
    count_key = jax.random.fold_in(key, 11)
    owner_key = jax.random.fold_in(key, 12)
    slot_key = jax.random.fold_in(key, 13)
    filled = jax.random.randint(count_key, (N_PB, N_PB), 1, CAP + 1)
    dest = jnp.arange(N_PB, dtype=jnp.int32)
    full_owner = (dest + 1) % N_PB
    filled = filled.at[full_owner, dest].set(CAP)
    device = jnp.arange(TRI_CAP * N_PB, dtype=jnp.int32) // TRI_CAP
    owner = jax.random.randint(owner_key, (TRI_CAP * N_PB,), 0, N_PB)
    limit = filled[owner, device]
    slot = jax.random.randint(slot_key, (TRI_CAP * N_PB,), 0, CAP) % limit
    return (owner * CAP + slot).astype(jnp.int32)


def draw_tri_count(key, part):
    count_key = jax.random.fold_in(key, 21)
    pick_key = jax.random.fold_in(key, 22)
    lowest = max(1, TRI_CAP // 2)
    counts = jax.random.randint(count_key, (N_PB,), lowest, TRI_CAP)
    busiest = jax.random.randint(pick_key, (), 0, N_PB)
    counts = counts.at[busiest].set(TRI_CAP)
    return counts.astype(jnp.int32)


def touch_ends(entries, rng, low, top_value):
    shape = entries.shape
    index_at = [jax.random.randint(jax.random.fold_in(rng, axis), (), 0, shape[axis]) for axis in range(len(shape))]
    entries = entries.at[tuple(index_at)].set(low)
    longest = shape.index(max(shape))
    index_at[longest] = (index_at[longest] + 1) % shape[longest]
    return entries.at[tuple(index_at)].set(top_value)


def block_levels(stream_key, shape, pieces, smallest, largest):
    def one(dim, shards_of):
        draws = jax.random.uniform(jax.random.fold_in(jax.random.fold_in(stream_key, 6), dim), (shards_of,), jnp.float32, smallest / len(pieces), largest / len(pieces))
        return jnp.repeat(jnp.exp(draws), shape[dim] // shards_of).reshape((-1,) + (1,) * (len(shape) - dim - 1))

    factor_of = one(*pieces[0])
    for cut in pieces[1:]:
        factor_of = factor_of * one(*cut)
    return factor_of


def centred(stream_key, shape, width, most, cuts=(), held_as=jnp.bfloat16):
    array = width * jax.random.normal(stream_key, shape, jnp.float32)
    if cuts:
        array = array * block_levels(stream_key, shape, cuts, -0.22, 0.18)
    return jnp.clip(array, -most, most).astype(held_as)


def setup_inputs(seed: int = 0, part: int = 0) -> dict:
    keys = jax.random.split(jax.random.key(seed), 9)
    own_keys = jax.random.split(jax.random.fold_in(keys[8], part), 9)
    return {
        "eigvec": centred(own_keys[0], (Q, 2 * NB * NB), 0.118, 0.69921875, ((0, 16),)),
        "omega": draw_omega(jax.random.fold_in(jax.random.fold_in(keys[8], part), 71), part),
        "phi": centred(keys[2], (NB, NB, NB), 1.0, 6.0),
        "send_rows": touch_ends(jax.random.randint(own_keys[3], (N_PB, N_PB * CAP), 0, QDEV), jax.random.fold_in(own_keys[3], 1), 0, QDEV - 1).astype(jnp.int32),
        "local_q": touch_ends(jax.random.randint(own_keys[4], (TRIPLETS,), 0, QDEV), jax.random.fold_in(own_keys[4], 1), 0, QDEV - 1).astype(jnp.int32),
        "partner_q": touch_ends(jax.random.randint(own_keys[5], (TRIPLETS,), 0, QDEV), jax.random.fold_in(own_keys[5], 1), 0, QDEV - 1).astype(jnp.int32),
        "slot_ref": draw_slot_ref(jax.random.fold_in(jax.random.fold_in(keys[8], part), 71), part),
        "tri_count": draw_tri_count(jax.random.fold_in(jax.random.fold_in(keys[8], part), 71), part),
    }


smear_width = 0.5


def triplet_rates(phi, near_vec, partner_vec, far_vec, near_freq, partner_freq, far_freq, weight_mask):
    phi_full = phi.astype(jnp.float32)
    far_real = far_vec[:, 0].astype(jnp.float32)
    far_imag = far_vec[:, 1].astype(jnp.float32)
    y_real = jnp.einsum('abc,tnc->tabn', phi_full, far_real)
    y_imag = -jnp.einsum('abc,tnc->tabn', phi_full, far_imag)
    y_real = y_real.astype(jnp.bfloat16).astype(jnp.float32)
    y_imag = y_imag.astype(jnp.bfloat16).astype(jnp.float32)
    part_real = partner_vec[:, 0].astype(jnp.float32)
    part_imag = partner_vec[:, 1].astype(jnp.float32)
    z_real = jnp.einsum('tmb,tabn->tamn', part_real, y_real) - jnp.einsum('tmb,tabn->tamn', part_imag, y_imag)
    z_imag = jnp.einsum('tmb,tabn->tamn', part_real, y_imag) + jnp.einsum('tmb,tabn->tamn', part_imag, y_real)
    z_real = z_real.astype(jnp.bfloat16).astype(jnp.float32)
    z_imag = z_imag.astype(jnp.bfloat16).astype(jnp.float32)
    near_real = near_vec[:, 0].astype(jnp.float32)
    near_imag = near_vec[:, 1].astype(jnp.float32)
    v_real = jnp.einsum('tva,tamn->tvmn', near_real, z_real) - jnp.einsum('tva,tamn->tvmn', near_imag, z_imag)
    v_imag = jnp.einsum('tva,tamn->tvmn', near_real, z_imag) + jnp.einsum('tva,tamn->tvmn', near_imag, z_real)
    power = v_real * v_real + v_imag * v_imag
    first = near_freq.astype(jnp.float32)[:, :, None, None]
    second = partner_freq.astype(jnp.float32)[:, None, :, None]
    third = far_freq.astype(jnp.float32)[:, None, None, :]
    offset = (first + second - third) / smear_width
    weight = jnp.exp(-offset * offset) / (first * second * third * NB)
    terms = power * weight * weight_mask[:, None, None, None]
    return jnp.sum(terms, axis=(2, 3)), jnp.sum(terms, axis=(1, 2))


def reference(eigvec, omega, phi, send_rows, local_q, partner_q, slot_ref, tri_count):
    total_q = QDEV * N_PB
    slot_index = jnp.arange(TRI_CAP * N_PB, dtype=jnp.int32)
    device = slot_index // TRI_CAP
    within = slot_index % TRI_CAP
    weight_mask = (within < tri_count[device]).astype(jnp.float32)
    owner = slot_ref // CAP
    column = device * CAP + slot_ref % CAP
    far_global = owner * QDEV + send_rows[owner, column]
    near_global = device * QDEV + local_q
    partner_global = device * QDEV + partner_q

    def one_device(packed):
        near_idx, partner_idx, far_idx, mask_part = packed
        near_vec = eigvec[near_idx].reshape(TRI_CAP, 2, NB, NB)
        partner_vec = eigvec[partner_idx].reshape(TRI_CAP, 2, NB, NB)
        far_vec = eigvec[far_idx].reshape(TRI_CAP, 2, NB, NB)
        return triplet_rates(phi, near_vec, partner_vec, far_vec, omega[near_idx], omega[partner_idx], omega[far_idx], mask_part)

    near_terms, far_terms = lax.map(one_device, (near_global.reshape(N_PB, TRI_CAP), partner_global.reshape(N_PB, TRI_CAP), far_global.reshape(N_PB, TRI_CAP), weight_mask.reshape(N_PB, TRI_CAP)))
    near_terms = near_terms.reshape(TRI_CAP * N_PB, NB)
    far_terms = far_terms.reshape(TRI_CAP * N_PB, NB)
    rates = jnp.zeros((NB, total_q), jnp.float32)
    rates = rates.at[:, near_global].add(near_terms.T)
    rates = rates.at[:, far_global].add(far_terms.T)
    return rates
```

```python
import functools

import jax
import jax.numpy as jnp
import numpy as np
from jax import lax
from jax.experimental import pallas as pl
from jax.experimental.pallas import tpu as pltpu
from jax.sharding import PartitionSpec as P

NB = 36
ROWS = 40
WIDE = 256
GROUPS = 6
smear_width = 0.5
F32, BF16 = jnp.float32, jnp.bfloat16
EXACT = lax.Precision.HIGHEST


def tables():
    start = [128 * h + 40 * u for h in range(2) for u in range(3)]
    spread_b = np.zeros((WIDE, NB), np.float32)
    spread_a = np.zeros((WIDE, NB), np.float32)
    pick = np.zeros((ROWS, WIDE), np.float32)
    own_two = np.full((WIDE,), -1)
    own_three = np.full((WIDE,), -2)
    column_two = np.full((WIDE,), -3)
    inner = np.full((WIDE,), -4)
    for block in range(GROUPS):
        for lane in range(NB):
            at = start[block] + lane
            outer, low = lane // GROUPS, lane % GROUPS
            spread_b[at, lane] = 1
            own_two[at] = block
            column_two[at] = outer
            spread_a[at, block * GROUPS + outer] = 1
            own_three[at] = low
            inner[at] = low
    for block in range(GROUPS):
        for lane in range(NB):
            pick[block * GROUPS + lane % GROUPS, start[block] + lane] = 1
    by_first = spread_a.T.copy()
    mask_two = (own_two[:, None] == column_two[None, :]).astype(np.float32)
    mask_three = (own_three[:, None] == inner[None, :]).astype(np.float32)
    second = np.zeros((GROUPS, NB, WIDE), np.float32)
    for group in range(GROUPS):
        for at in range(WIDE):
            if inner[at] >= 0:
                second[group, group * GROUPS + inner[at], at] = 1
    both_two = np.zeros((2 * ROWS, 2 * WIDE), np.float32)
    both_two[:ROWS, :WIDE] = pick
    both_two[ROWS:, WIDE:] = pick
    both_three = np.zeros((2 * ROWS, 2 * WIDE), np.float32)
    both_three[:NB, :WIDE] = by_first
    both_three[ROWS : ROWS + NB, WIDE:] = by_first
    by_first_rows = np.zeros((ROWS, WIDE), np.float32)
    by_first_rows[:NB] = by_first
    eye = np.zeros((ROWS, NB), np.float32)
    eye[:NB] = np.eye(NB)
    return dict(
        spread_b=spread_b.astype(BF16),
        spread_a=spread_a.astype(BF16),
        both_two=both_two.astype(BF16),
        both_three=both_three.astype(BF16),
        mask_two=mask_two,
        mask_three=mask_three,
        first=by_first.astype(BF16),
        second=np.transpose(second, (1, 0, 2)).reshape(NB, GROUPS * WIDE).astype(BF16),
        first_rows=by_first_rows,
        eye=eye.astype(BF16),
    )


NAMES = (
    "spread_b", "spread_a", "both_two", "both_three", "mask_two",
    "mask_three", "first", "second", "first_rows", "eye",
)


def nt(left, right, precision=None):
    return lax.dot_general(
        left, right, (((1,), (1,)), ((), ())),
        preferred_element_type=F32, precision=precision,
    )


def nn(left, right, precision=None):
    return jnp.dot(left, right, preferred_element_type=F32, precision=precision)


def contract_kernel(
    phi, near, partner, far, near_freq, partner_freq, far_freq, near_col, slot_row, live,
    spread_b, spread_a, both_two, both_three, mask_two, mask_three, first, second,
    first_rows, eye, rates, by_slot, y_all, z_all, w_first, w_second, w_third, near_acc,
):
    slots = near.shape[0]
    for group in range(GROUPS):
        force = phi[pl.ds(group * WIDE, WIDE), :]

        def fill(t, carry):
            y_all[t, group] = nt(far[t], force).astype(BF16)
            return carry

        lax.fori_loop(0, slots, fill, 0, unroll=4)
    w_first[...] = nn(near_freq[...], first[...])
    w_second[...] = nn(partner_freq[...], second[...])
    third = nt(eye[...], far_freq[...])
    for t in range(slots):
        w_third[t] = jnp.broadcast_to(third[:, t : t + 1], (ROWS, WIDE))
    lane = lax.broadcasted_iota(jnp.int32, (2 * ROWS, 128), 1)
    column = lax.broadcasted_iota(jnp.int32, (1, 128), 1)
    wide_lane = lax.broadcasted_iota(jnp.int32, (1, WIDE), 1) % 128
    block = wide_lane % 40
    used = (block < NB) & (wide_lane < 120)

    def one(t, far_cols):
        spread = nt(spread_b[...], partner[t]).astype(BF16)
        two = (nn(spread, both_two[...]) * jnp.concatenate([mask_two[...]] * 2, 1)).astype(BF16)
        spread = nt(spread_a[...], near[t]).astype(BF16)
        three = (nn(spread, both_three[...]) * jnp.concatenate([mask_three[...]] * 2, 1)).astype(BF16)
        for group in range(GROUPS):
            part = nn(y_all[t, group], two)
            real = part[:ROWS, :WIDE] - part[ROWS:, WIDE:]
            imag = part[:ROWS, WIDE:] + part[ROWS:, :WIDE]
            z_all[group] = jnp.concatenate([real, imag], 0)
        w1 = w_first[pl.ds(t, 1), :]
        w3 = w_third[t]
        inv_third = jnp.where(w3 > 0, 1.0 / w3, 0.0)
        total = jnp.zeros((ROWS, WIDE), F32)
        for group in range(GROUPS):
            half, place = divmod(group, 3)
            tiles = []
            for out_half in range(2):
                pieces = []
                for out_place in range(3):
                    piece = z_all[3 * out_half + out_place, :, pl.ds(128 * half, 128)]
                    shift = (40 * (out_place - place)) % 128
                    pieces.append(pltpu.roll(piece, shift, 1) if shift else piece)
                tiles.append(
                    jnp.where(
                        lane < 40,
                        pieces[0],
                        jnp.where(lane < 80, pieces[1], jnp.where(lane < 120, pieces[2], 0.0)),
                    )
                )
            part = nn(jnp.concatenate(tiles, 1).astype(BF16), three)
            real = part[:ROWS, :WIDE] - part[ROWS:, WIDE:]
            imag = part[:ROWS, WIDE:] + part[ROWS:, :WIDE]
            power = real * real + imag * imag
            w2 = w_second[pl.ds(t, 1), pl.ds(group * WIDE, WIDE)]
            offset = ((w1 + w2) - w3) * (1.0 / smear_width)
            inverse = jnp.where(used, 1.0 / jnp.where(used, w1 * w2 * NB, 1.0), 0.0)
            total = total + power * jnp.exp(-offset * offset) * inverse
        total = total * inv_third
        alive = (t < live[0]).astype(F32)
        near_acc[pl.ds(t, 1), :] = jnp.sum(total, axis=0, keepdims=True) * alive
        sums = jnp.sum(total, axis=1, keepdims=True) * alive
        return far_cols + jnp.where(column == t, sums, 0.0)

    far_cols = lax.fori_loop(0, slots, one, jnp.zeros((ROWS, 128), F32))
    near_cols = nt(first_rows[...], near_acc[...], EXACT)
    q_count = rates.shape[1]
    to_q = (
        lax.broadcasted_iota(jnp.int32, (slots, q_count), 1) == near_col[...]
    ).astype(F32)
    rates[...] = nn(near_cols, to_q, EXACT)[:NB]
    to_slot = (
        lax.broadcasted_iota(jnp.int32, (by_slot.shape[0], slots), 0) == slot_row[...]
    ).astype(F32)
    by_slot[...] = nt(to_slot, far_cols[:, :slots], EXACT)[:, :NB]


def finish_kernel(rates, returned, rows, out):
    slots, q_count = returned.shape[0], rates.shape[1]
    eye = (
        lax.broadcasted_iota(jnp.int32, (ROWS, NB), 0)
        == lax.broadcasted_iota(jnp.int32, (ROWS, NB), 1)
    ).astype(F32)
    back = nt(eye, returned[...], EXACT)
    to_q = (lax.broadcasted_iota(jnp.int32, (slots, q_count), 1) == rows[...]).astype(F32)
    out[...] = rates[...] + nn(back, to_q, EXACT)[:NB]


def as_rows(vecs):
    count = vecs.shape[0]
    parts = vecs.reshape(count, 2, NB, NB)
    return jnp.pad(parts, ((0, 0), (0, 0), (0, ROWS - NB), (0, 0))).reshape(count, 2 * ROWS, NB)


def take(array, rows):
    return array.at[rows].get(mode="promise_in_bounds")


def on_device(eigvec, omega, phi, send_rows, local_q, partner_q, slot_ref, tri_count):
    owned = eigvec.shape[0]
    outgoing = send_rows[0]
    slots = local_q.shape[0]
    sent = jnp.concatenate([take(eigvec, outgoing), take(omega, outgoing)], 1)
    arrived = lax.all_to_all(sent, "pb", split_axis=0, concat_axis=0, tiled=True)
    force = jnp.pad(
        jnp.pad(phi, ((0, 0), (0, ROWS - NB), (0, 0))).reshape(2 * GROUPS, 3 * ROWS, NB),
        ((0, 0), (0, 8), (0, 0)),
    ).reshape(GROUPS * WIDE, NB)
    far_pair = take(arrived, slot_ref)
    far = as_rows(far_pair[:, : 2 * NB * NB])
    sign = jnp.where(jnp.arange(2 * ROWS) < ROWS, 1, -1).astype(BF16)
    far = far * sign[None, :, None]
    held = tables()
    vmem = pl.BlockSpec(memory_space=pltpu.VMEM)
    rates, by_slot = pl.pallas_call(
        contract_kernel,
        out_shape=(
            jax.ShapeDtypeStruct((NB, owned), F32),
            jax.ShapeDtypeStruct((outgoing.shape[0], NB), F32),
        ),
        in_specs=[vmem] * 9 + [pl.BlockSpec(memory_space=pltpu.SMEM)] + [vmem] * len(NAMES),
        out_specs=(vmem, vmem),
        scratch_shapes=[
            pltpu.VMEM((slots, GROUPS, 2 * ROWS, WIDE), BF16),
            pltpu.VMEM((GROUPS, 2 * ROWS, WIDE), F32),
            pltpu.VMEM((slots, WIDE), F32),
            pltpu.VMEM((slots, GROUPS * WIDE), F32),
            pltpu.VMEM((slots, ROWS, WIDE), F32),
            pltpu.VMEM((slots, WIDE), F32),
        ],
        compiler_params=pltpu.CompilerParams(vmem_limit_bytes=48 * 2**20),
    )(
        force,
        as_rows(take(eigvec, local_q)),
        as_rows(take(eigvec, partner_q)),
        far,
        take(omega, local_q),
        take(omega, partner_q),
        far_pair[:, 2 * NB * NB :],
        local_q[:, None],
        slot_ref[None, :],
        tri_count,
        *[jnp.asarray(held[name]) for name in NAMES],
    )
    returned = lax.all_to_all(by_slot, "pb", split_axis=0, concat_axis=0, tiled=True)
    return pl.pallas_call(
        finish_kernel,
        out_shape=jax.ShapeDtypeStruct((NB, owned), F32),
        in_specs=[vmem] * 3,
        out_specs=vmem,
    )(rates, returned, outgoing[:, None])


def solution(mesh):
    split = P(("groups", "pb"))
    rows = P(("groups", "pb"), None)
    return jax.shard_map(
        on_device,
        mesh=mesh,
        in_specs=(rows, rows, P(), rows, split, split, split, split),
        out_specs=P(None, ("groups", "pb")),
        check_vma=False,
    )
```

```python
import functools

import jax
import jax.numpy as jnp
import numpy as np
from jax import lax
from jax.experimental import pallas as pl
from jax.experimental.pallas import tpu as pltpu
from jax.sharding import PartitionSpec as P

NB = 36
ROWS = 40
WIDE = 256
GROUPS = 6
smear_width = 0.5
F32, BF16 = jnp.float32, jnp.bfloat16
EXACT = lax.Precision.HIGHEST


def tables():
    start = [128 * h + 40 * u for h in range(2) for u in range(3)]
    spread_b = np.zeros((WIDE, NB), np.float32)
    spread_a = np.zeros((WIDE, NB), np.float32)
    pick = np.zeros((ROWS, WIDE), np.float32)
    own_two = np.full((WIDE,), -1)
    own_three = np.full((WIDE,), -2)
    column_two = np.full((WIDE,), -3)
    inner = np.full((WIDE,), -4)
    for block in range(GROUPS):
        for lane in range(NB):
            at = start[block] + lane
            outer, low = lane // GROUPS, lane % GROUPS
            spread_b[at, lane] = 1
            own_two[at] = block
            column_two[at] = outer
            spread_a[at, block * GROUPS + outer] = 1
            own_three[at] = low
            inner[at] = low
    for block in range(GROUPS):
        for lane in range(NB):
            pick[block * GROUPS + lane % GROUPS, start[block] + lane] = 1
    by_first = spread_a.T.copy()
    mask_two = (own_two[:, None] == column_two[None, :]).astype(np.float32)
    mask_three = (own_three[:, None] == inner[None, :]).astype(np.float32)
    second = np.zeros((GROUPS, NB, WIDE), np.float32)
    for group in range(GROUPS):
        for at in range(WIDE):
            if inner[at] >= 0:
                second[group, group * GROUPS + inner[at], at] = 1
    lift_b = np.zeros((2, WIDE, 128), np.float32)
    lift_a = np.zeros((2, WIDE, 128), np.float32)
    for part in range(2):
        lift_b[part, :, part * NB : (part + 1) * NB] = spread_b
        lift_a[part, :, part * NB : (part + 1) * NB] = spread_a
    by_first_rows = np.zeros((ROWS, WIDE), np.float32)
    by_first_rows[:NB] = by_first
    return dict(
        spread_b=lift_b.astype(BF16),
        spread_a=lift_a.astype(BF16),
        both_two=pick.astype(BF16),
        both_three=by_first_rows.astype(BF16),
        mask_two=mask_two.astype(BF16),
        mask_three=mask_three.astype(BF16),
        first=by_first.astype(BF16),
        second=np.transpose(second, (1, 0, 2)).reshape(NB, GROUPS * WIDE).astype(BF16),
        first_rows=by_first_rows,
    )


NAMES = (
    "spread_b", "spread_a", "both_two", "both_three", "mask_two",
    "mask_three", "first", "second", "first_rows",
)


def nt(left, right, precision=None):
    return lax.dot_general(
        left, right, (((1,), (1,)), ((), ())),
        preferred_element_type=F32, precision=precision,
    )


def nn(left, right, precision=None):
    return jnp.dot(left, right, preferred_element_type=F32, precision=precision)


def peers(count):
    me = lax.axis_index("pb")

    def at(step):
        return lax.rem(me + step, count)

    return me, at


def greet(count):
    _, at = peers(count)
    barrier = pltpu.get_barrier_semaphore()

    def signal(step, carry):
        pl.semaphore_signal(
            barrier, inc=1, device_id={"pb": at(step)}, device_id_type=pl.DeviceIdType.MESH
        )
        return carry

    lax.fori_loop(1, count, signal, 0)
    pl.semaphore_wait(barrier, count - 1)


def exchange(count, source, target, send_sem, recv_sem):
    me, at = peers(count)

    def copy(peer, slot):
        return pltpu.make_async_remote_copy(
            src_ref=source.at[peer],
            dst_ref=target.at[slot],
            send_sem=send_sem.at[peer],
            recv_sem=recv_sem.at[slot],
            device_id={"pb": peer},
            device_id_type=pl.DeviceIdType.MESH,
        )

    def start(step, carry):
        copy(at(step), me).start()
        return carry

    def finish(step, carry):
        copy(at(step), at(step)).wait_recv()
        return carry

    def drain(step, carry):
        copy(at(step), me).wait_send()
        return carry

    return (
        lambda: lax.fori_loop(1, count, start, 0),
        lambda: lax.fori_loop(1, count, finish, 0),
        lambda: lax.fori_loop(1, count, drain, 0),
    )


def contract_kernel(
    count, cap, slot_ref, live, outgoing, near, partner, force, near_freq, partner_freq,
    near_col, slot_row, spread_b, spread_a, both_two, both_three, mask_two, mask_three,
    first, second, first_rows, rates, by_slot, arrived, two_all, three_all, y_all, z_all,
    w_first, w_second, w_third, near_acc, send_sem, recv_sem,
):
    slots = near.shape[0]
    me, _ = peers(count)
    start, finish, drain = exchange(count, outgoing, arrived, send_sem, recv_sem)
    greet(count)
    start()
    arrived[me] = outgoing[me]

    w_first[...] = nn(near_freq[...], first[...])
    w_second[...] = nn(partner_freq[...], second[...])

    def prepare(t, carry):
        for own, spread, picks, mask, held in (
            (partner, spread_b, both_two, mask_two, two_all),
            (near, spread_a, both_three, mask_three, three_all),
        ):
            vecs = own[t]
            for part in range(2):
                lifted = nt(spread[part], vecs).astype(BF16)
                held[t, :, pl.ds(part * WIDE, WIDE)] = (
                    nn(lifted, picks[...]).astype(BF16) * mask[...]
                )
        return carry

    lax.fori_loop(0, slots, prepare, 0, unroll=2)
    finish()

    def fill(t, carry):
        far = arrived[slot_ref[t] // cap, slot_ref[t] % cap]
        w_third[t] = jnp.broadcast_to(far[:, 2 * NB : 2 * NB + 1].astype(F32), (ROWS, WIDE))
        for group in range(GROUPS):
            for part in range(2):
                rows = pl.ds(part * ROWS, ROWS)
                tile = force[part, pl.ds(group * WIDE, WIDE), :]
                y_all[t, group, rows] = nt(far, tile).astype(BF16)
        return carry

    lax.fori_loop(0, slots, fill, 0, unroll=2)
    lane = lax.broadcasted_iota(jnp.int32, (2 * ROWS, 128), 1)
    column = lax.broadcasted_iota(jnp.int32, (1, 128), 1)
    wide_lane = lax.broadcasted_iota(jnp.int32, (1, WIDE), 1) % 128
    used = (wide_lane % 40 < NB) & (wide_lane < 120)

    def one(t, far_cols):
        two = two_all[t]
        three = three_all[t]
        for group in range(GROUPS):
            part = nn(y_all[t, group], two)
            real = part[:ROWS, :WIDE] - part[ROWS:, WIDE:]
            imag = part[:ROWS, WIDE:] + part[ROWS:, :WIDE]
            z_all[group] = jnp.concatenate([real, imag], 0)
        w1 = w_first[pl.ds(t, 1), :]
        w3 = w_third[t]
        inv_third = jnp.where(w3 > 0, 1.0 / w3, 0.0)
        total = jnp.zeros((ROWS, WIDE), F32)
        for group in range(GROUPS):
            half, place = divmod(group, 3)
            tiles = []
            for out_half in range(2):
                pieces = []
                for out_place in range(3):
                    piece = z_all[3 * out_half + out_place, :, pl.ds(128 * half, 128)]
                    shift = (40 * (out_place - place)) % 128
                    pieces.append(pltpu.roll(piece, shift, 1) if shift else piece)
                tiles.append(
                    jnp.where(
                        lane < 40,
                        pieces[0],
                        jnp.where(lane < 80, pieces[1], jnp.where(lane < 120, pieces[2], 0.0)),
                    )
                )
            part = nn(jnp.concatenate(tiles, 1).astype(BF16), three)
            real = part[:ROWS, :WIDE] - part[ROWS:, WIDE:]
            imag = part[:ROWS, WIDE:] + part[ROWS:, :WIDE]
            power = real * real + imag * imag
            w2 = w_second[pl.ds(t, 1), pl.ds(group * WIDE, WIDE)]
            offset = ((w1 + w2) - w3) * (1.0 / smear_width)
            inverse = jnp.where(used, 1.0 / jnp.where(used, w1 * w2 * NB, 1.0), 0.0)
            total = total + power * jnp.exp(-offset * offset) * inverse
        total = total * inv_third
        alive = (t < live[0]).astype(F32)
        near_acc[pl.ds(t, 1), :] = jnp.sum(total, axis=0, keepdims=True) * alive
        sums = jnp.sum(total, axis=1, keepdims=True) * alive
        return far_cols + jnp.where(column == t, sums, 0.0)

    far_cols = lax.fori_loop(0, slots, one, jnp.zeros((ROWS, 128), F32))
    near_cols = nt(first_rows[...], near_acc[...], EXACT)
    q_count = rates.shape[1]
    to_q = (
        lax.broadcasted_iota(jnp.int32, (slots, q_count), 1) == near_col[...]
    ).astype(F32)
    rates[...] = nn(near_cols, to_q, EXACT)[:NB]
    to_slot = (
        lax.broadcasted_iota(jnp.int32, (count * cap, slots), 0) == slot_row[...]
    ).astype(F32)
    sums = nt(to_slot, far_cols[:, :slots], EXACT)[:, :NB]
    for owner in range(count):
        by_slot[owner] = sums[owner * cap : (owner + 1) * cap]
    drain()


def finish_kernel(count, rates, sent, rows, out, returned, send_sem, recv_sem):
    me, _ = peers(count)
    start, finish, drain = exchange(count, sent, returned, send_sem, recv_sem)
    greet(count)
    start()
    returned[me] = sent[me]
    slots, q_count = rows.shape[0], rates.shape[1]
    eye = (
        lax.broadcasted_iota(jnp.int32, (ROWS, NB), 0)
        == lax.broadcasted_iota(jnp.int32, (ROWS, NB), 1)
    ).astype(F32)
    to_q = (lax.broadcasted_iota(jnp.int32, (slots, q_count), 1) == rows[...]).astype(F32)
    finish()
    back = nt(eye, jnp.concatenate([returned[owner] for owner in range(count)], 0), EXACT)
    out[...] = rates[...] + nn(back, to_q, EXACT)[:NB]
    drain()


def take(array, rows):
    return array.at[rows].get(mode="promise_in_bounds")


def on_device(eigvec, omega, phi, send_rows, local_q, partner_q, slot_ref, tri_count):
    owned = eigvec.shape[0]
    outgoing = send_rows[0]
    slots = local_q.shape[0]
    count = lax.axis_size("pb")
    cap = outgoing.shape[0] // count
    sent = outgoing.shape[0]
    wanted = jnp.concatenate([outgoing, local_q, partner_q])
    vecs = take(eigvec, wanted).reshape(-1, 2, NB, NB)
    freqs = take(omega, wanted)
    packed = jnp.concatenate([vecs[:, 0], vecs[:, 1], freqs[:, :, None]], 2)
    packed = jnp.pad(packed, ((0, 0), (0, ROWS - NB), (0, 127 - 2 * NB)))
    tiles = jnp.pad(
        jnp.pad(phi, ((0, 0), (0, ROWS - NB), (0, 0))).reshape(2 * GROUPS, 3 * ROWS, NB),
        ((0, 0), (0, 8), (0, 0)),
    ).reshape(GROUPS * WIDE, NB)
    force = jnp.stack(
        [
            jnp.pad(tiles, ((0, 0), (0, 128 - NB))),
            jnp.pad(-tiles, ((0, 0), (NB, 128 - 2 * NB))),
        ]
    )
    held = tables()
    vmem = pl.BlockSpec(memory_space=pltpu.VMEM)
    smem = pl.BlockSpec(memory_space=pltpu.SMEM)
    rates, by_slot = pl.pallas_call(
        functools.partial(contract_kernel, count, cap),
        out_shape=(
            jax.ShapeDtypeStruct((NB, owned), F32),
            jax.ShapeDtypeStruct((count, cap, NB), F32),
        ),
        in_specs=[smem] * 2 + [vmem] * (8 + len(NAMES)),
        out_specs=(vmem, vmem),
        scratch_shapes=[
            pltpu.VMEM((count, cap, ROWS, 128), BF16),
            pltpu.VMEM((slots, WIDE, 2 * WIDE), BF16),
            pltpu.VMEM((slots, WIDE, 2 * WIDE), BF16),
            pltpu.VMEM((slots, GROUPS, 2 * ROWS, WIDE), BF16),
            pltpu.VMEM((GROUPS, 2 * ROWS, WIDE), F32),
            pltpu.VMEM((slots, WIDE), F32),
            pltpu.VMEM((slots, GROUPS * WIDE), F32),
            pltpu.VMEM((slots, ROWS, WIDE), F32),
            pltpu.VMEM((slots, WIDE), F32),
            pltpu.SemaphoreType.DMA((count,)),
            pltpu.SemaphoreType.DMA((count,)),
        ],
        compiler_params=pltpu.CompilerParams(
            vmem_limit_bytes=48 * 2**20, collective_id=0, has_side_effects=True
        ),
    )(
        slot_ref,
        tri_count,
        packed[:sent].reshape(count, cap, ROWS, 128),
        packed[sent : sent + slots],
        packed[sent + slots :],
        force,
        freqs[sent : sent + slots],
        freqs[sent + slots :],
        local_q[:, None],
        slot_ref[None, :],
        *[jnp.asarray(held[name]) for name in NAMES],
    )
    return pl.pallas_call(
        functools.partial(finish_kernel, count),
        out_shape=jax.ShapeDtypeStruct((NB, owned), F32),
        in_specs=[vmem] * 3,
        out_specs=vmem,
        scratch_shapes=[
            pltpu.VMEM((count, cap, NB), F32),
            pltpu.SemaphoreType.DMA((count,)),
            pltpu.SemaphoreType.DMA((count,)),
        ],
        compiler_params=pltpu.CompilerParams(collective_id=1, has_side_effects=True),
    )(rates, by_slot, outgoing[:, None])


def solution(mesh):
    split = P(("groups", "pb"))
    rows = P(("groups", "pb"), None)
    return jax.shard_map(
        on_device,
        mesh=mesh,
        in_specs=(rows, rows, P(), rows, split, split, split, split),
        out_specs=P(None, ("groups", "pb")),
        check_vma=False,
    )
```

```python
import functools

import jax
import jax.numpy as jnp
import numpy as np
from jax import lax
from jax.experimental import pallas as pl
from jax.experimental.pallas import tpu as pltpu
from jax.sharding import PartitionSpec as P

NB = 36
ROWS = 40
WIDE = 256
GROUPS = 6
smear_width = 0.5
F32, BF16 = jnp.float32, jnp.bfloat16
EXACT = lax.Precision.HIGHEST


def tables():
    start = [128 * h + 40 * u for h in range(2) for u in range(3)]
    spread_b = np.zeros((WIDE, NB), np.float32)
    spread_a = np.zeros((WIDE, NB), np.float32)
    pick = np.zeros((ROWS, WIDE), np.float32)
    own_two = np.full((WIDE,), -1)
    own_three = np.full((WIDE,), -2)
    column_two = np.full((WIDE,), -3)
    inner = np.full((WIDE,), -4)
    for block in range(GROUPS):
        for lane in range(NB):
            at = start[block] + lane
            outer, low = lane // GROUPS, lane % GROUPS
            spread_b[at, lane] = 1
            own_two[at] = block
            column_two[at] = outer
            spread_a[at, block * GROUPS + outer] = 1
            own_three[at] = low
            inner[at] = low
    for block in range(GROUPS):
        for lane in range(NB):
            pick[block * GROUPS + lane % GROUPS, start[block] + lane] = 1
    by_first = spread_a.T.copy()
    mask_two = (own_two[:, None] == column_two[None, :]).astype(np.float32)
    mask_three = (own_three[:, None] == inner[None, :]).astype(np.float32)
    second = np.zeros((GROUPS, NB, WIDE), np.float32)
    for group in range(GROUPS):
        for at in range(WIDE):
            if inner[at] >= 0:
                second[group, group * GROUPS + inner[at], at] = 1
    lift_b = np.zeros((2, WIDE, 128), np.float32)
    lift_a = np.zeros((2, WIDE, 128), np.float32)
    for part in range(2):
        lift_b[part, :, part * NB : (part + 1) * NB] = spread_b
        lift_a[part, :, part * NB : (part + 1) * NB] = spread_a
    by_first_rows = np.zeros((ROWS, WIDE), np.float32)
    by_first_rows[:NB] = by_first
    return dict(
        spread_b=lift_b.astype(BF16),
        spread_a=lift_a.astype(BF16),
        both_two=pick.astype(BF16),
        both_three=by_first_rows.astype(BF16),
        mask_two=mask_two.astype(BF16),
        mask_three=mask_three.astype(BF16),
        first=by_first.astype(BF16),
        second=np.transpose(second, (1, 0, 2)).reshape(NB, GROUPS * WIDE).astype(BF16),
        first_rows=by_first_rows,
    )


NAMES = (
    "spread_b", "spread_a", "both_two", "both_three", "mask_two",
    "mask_three", "first", "second", "first_rows",
)


def nt(left, right, precision=None):
    return lax.dot_general(
        left, right, (((1,), (1,)), ((), ())),
        preferred_element_type=F32, precision=precision,
    )


def nn(left, right, precision=None):
    return jnp.dot(left, right, preferred_element_type=F32, precision=precision)


def peers(count):
    me = lax.axis_index("pb")

    def at(step):
        return lax.rem(me + step, count)

    return me, at


def greet(count):
    _, at = peers(count)
    barrier = pltpu.get_barrier_semaphore()

    def signal(step, carry):
        pl.semaphore_signal(
            barrier, inc=1, device_id={"pb": at(step)}, device_id_type=pl.DeviceIdType.MESH
        )
        return carry

    lax.fori_loop(1, count, signal, 0)
    pl.semaphore_wait(barrier, count - 1)


def exchange(count, source, target, send_sem, recv_sem):
    me, at = peers(count)

    def copy(peer, slot):
        return pltpu.make_async_remote_copy(
            src_ref=source.at[peer],
            dst_ref=target.at[slot],
            send_sem=send_sem.at[peer],
            recv_sem=recv_sem.at[slot],
            device_id={"pb": peer},
            device_id_type=pl.DeviceIdType.MESH,
        )

    def start(step, carry):
        copy(at(step), me).start()
        return carry

    def finish(step, carry):
        copy(at(step), at(step)).wait_recv()
        return carry

    def drain(step, carry):
        copy(at(step), me).wait_send()
        return carry

    return (
        lambda: lax.fori_loop(1, count, start, 0),
        lambda: lax.fori_loop(1, count, finish, 0),
        lambda: lax.fori_loop(1, count, drain, 0),
    )


def contract_kernel(
    count, cap, slot_ref, live, outgoing, near, partner, force, near_freq, partner_freq,
    near_col, slot_row, spread_b, spread_a, both_two, both_three, mask_two, mask_three,
    first, second, first_rows, rates, by_slot, arrived, two_all, three_all, y_all, z_all,
    w_first, w_second, w_third, near_acc, far_all, x_all, send_sem, recv_sem,
):
    slots = near.shape[0]
    me, _ = peers(count)
    start, finish, drain = exchange(count, outgoing, arrived, send_sem, recv_sem)
    greet(count)
    start()
    arrived[me] = outgoing[me]

    w_first[...] = nn(near_freq[...], first[...])
    w_second[...] = nn(partner_freq[...], second[...])

    def prepare(t, carry):
        for own, spread, picks, mask, held in (
            (partner, spread_b, both_two, mask_two, two_all),
            (near, spread_a, both_three, mask_three, three_all),
        ):
            vecs = own[t]
            for part in range(2):
                lifted = nt(spread[part], vecs).astype(BF16)
                held[t, :, pl.ds(part * WIDE, WIDE)] = (
                    nn(lifted, picks[...]).astype(BF16) * mask[...]
                )
        return carry

    lax.fori_loop(0, slots, prepare, 0, unroll=2)
    finish()

    def fill(t, carry):
        far = arrived[slot_ref[t] // cap, slot_ref[t] % cap]
        w_third[t] = jnp.broadcast_to(far[:, 2 * NB : 2 * NB + 1].astype(F32), (ROWS, WIDE))
        far_all[t] = far.astype(F32)
        return carry

    lax.fori_loop(0, slots, fill, 0, unroll=2)
    fars = far_all[...].reshape(slots * ROWS, 128).astype(BF16)
    for group in range(GROUPS):
        for part in range(2):
            made = nt(fars, force[part, pl.ds(group * WIDE, WIDE), :])
            y_all[:, group, pl.ds(part * ROWS, ROWS), :] = made.reshape(
                slots, ROWS, WIDE
            ).astype(BF16)
    lane = lax.broadcasted_iota(jnp.int32, (2 * ROWS, 128), 1)
    column = lax.broadcasted_iota(jnp.int32, (1, 128), 1)
    wide_lane = lax.broadcasted_iota(jnp.int32, (1, WIDE), 1) % 128
    used = (wide_lane % 40 < NB) & (wide_lane < 120)

    def one(t, far_cols):
        two = two_all[t]
        three = three_all[t]
        made = nn(y_all[t].reshape(GROUPS * 2 * ROWS, WIDE), two)
        for group in range(GROUPS):
            part = made[group * 2 * ROWS : (group + 1) * 2 * ROWS]
            real = part[:ROWS, :WIDE] - part[ROWS:, WIDE:]
            imag = part[:ROWS, WIDE:] + part[ROWS:, :WIDE]
            z_all[group] = jnp.concatenate([real, imag], 0)
        w1 = w_first[pl.ds(t, 1), :]
        w3 = w_third[t]
        inv_third = jnp.where(w3 > 0, 1.0 / w3, 0.0)
        total = jnp.zeros((ROWS, WIDE), F32)
        for group in range(GROUPS):
            half, place = divmod(group, 3)
            tiles = []
            for out_half in range(2):
                pieces = []
                for out_place in range(3):
                    piece = z_all[3 * out_half + out_place, :, pl.ds(128 * half, 128)]
                    shift = (40 * (out_place - place)) % 128
                    pieces.append(pltpu.roll(piece, shift, 1) if shift else piece)
                tiles.append(
                    jnp.where(
                        lane < 40,
                        pieces[0],
                        jnp.where(lane < 80, pieces[1], jnp.where(lane < 120, pieces[2], 0.0)),
                    )
                )
            x_all[group] = jnp.concatenate(tiles, 1).astype(BF16)
        made = nn(x_all[...].reshape(GROUPS * 2 * ROWS, WIDE), three)
        for group in range(GROUPS):
            part = made[group * 2 * ROWS : (group + 1) * 2 * ROWS]
            real = part[:ROWS, :WIDE] - part[ROWS:, WIDE:]
            imag = part[:ROWS, WIDE:] + part[ROWS:, :WIDE]
            power = real * real + imag * imag
            w2 = w_second[pl.ds(t, 1), pl.ds(group * WIDE, WIDE)]
            offset = ((w1 + w2) - w3) * (1.0 / smear_width)
            inverse = jnp.where(used, 1.0 / jnp.where(used, w1 * w2 * NB, 1.0), 0.0)
            total = total + power * jnp.exp(-offset * offset) * inverse
        total = total * inv_third
        alive = (t < live[0]).astype(F32)
        near_acc[pl.ds(t, 1), :] = jnp.sum(total, axis=0, keepdims=True) * alive
        sums = jnp.sum(total, axis=1, keepdims=True) * alive
        return far_cols + jnp.where(column == t, sums, 0.0)

    far_cols = lax.fori_loop(0, slots, one, jnp.zeros((ROWS, 128), F32))
    near_cols = nt(first_rows[...], near_acc[...], EXACT)
    q_count = rates.shape[1]
    to_q = (
        lax.broadcasted_iota(jnp.int32, (slots, q_count), 1) == near_col[...]
    ).astype(F32)
    rates[...] = nn(near_cols, to_q, EXACT)[:NB]
    to_slot = (
        lax.broadcasted_iota(jnp.int32, (count * cap, slots), 0) == slot_row[...]
    ).astype(F32)
    sums = nt(to_slot, far_cols[:, :slots], EXACT)[:, :NB]
    for owner in range(count):
        by_slot[owner] = sums[owner * cap : (owner + 1) * cap]
    drain()


def finish_kernel(count, rates, sent, rows, out, returned, send_sem, recv_sem):
    me, _ = peers(count)
    start, finish, drain = exchange(count, sent, returned, send_sem, recv_sem)
    greet(count)
    start()
    returned[me] = sent[me]
    slots, q_count = rows.shape[0], rates.shape[1]
    eye = (
        lax.broadcasted_iota(jnp.int32, (ROWS, NB), 0)
        == lax.broadcasted_iota(jnp.int32, (ROWS, NB), 1)
    ).astype(F32)
    to_q = (lax.broadcasted_iota(jnp.int32, (slots, q_count), 1) == rows[...]).astype(F32)
    finish()
    back = nt(eye, jnp.concatenate([returned[owner] for owner in range(count)], 0), EXACT)
    out[...] = rates[...] + nn(back, to_q, EXACT)[:NB]
    drain()


def take(array, rows):
    return array.at[rows].get(mode="promise_in_bounds")


def on_device(eigvec, omega, phi, send_rows, local_q, partner_q, slot_ref, tri_count):
    owned = eigvec.shape[0]
    outgoing = send_rows[0]
    slots = local_q.shape[0]
    count = lax.axis_size("pb")
    cap = outgoing.shape[0] // count
    sent = outgoing.shape[0]
    wanted = jnp.concatenate([outgoing, local_q, partner_q])
    vecs = take(eigvec, wanted).reshape(-1, 2, NB, NB)
    freqs = take(omega, wanted)
    packed = jnp.concatenate([vecs[:, 0], vecs[:, 1], freqs[:, :, None]], 2)
    packed = jnp.pad(packed, ((0, 0), (0, ROWS - NB), (0, 127 - 2 * NB)))
    tiles = jnp.pad(
        jnp.pad(phi, ((0, 0), (0, ROWS - NB), (0, 0))).reshape(2 * GROUPS, 3 * ROWS, NB),
        ((0, 0), (0, 8), (0, 0)),
    ).reshape(GROUPS * WIDE, NB)
    force = jnp.stack(
        [
            jnp.pad(tiles, ((0, 0), (0, 128 - NB))),
            jnp.pad(-tiles, ((0, 0), (NB, 128 - 2 * NB))),
        ]
    )
    held = tables()
    vmem = pl.BlockSpec(memory_space=pltpu.VMEM)
    smem = pl.BlockSpec(memory_space=pltpu.SMEM)
    rates, by_slot = pl.pallas_call(
        functools.partial(contract_kernel, count, cap),
        out_shape=(
            jax.ShapeDtypeStruct((NB, owned), F32),
            jax.ShapeDtypeStruct((count, cap, NB), F32),
        ),
        in_specs=[smem] * 2 + [vmem] * (8 + len(NAMES)),
        out_specs=(vmem, vmem),
        scratch_shapes=[
            pltpu.VMEM((count, cap, ROWS, 128), BF16),
            pltpu.VMEM((slots, WIDE, 2 * WIDE), BF16),
            pltpu.VMEM((slots, WIDE, 2 * WIDE), BF16),
            pltpu.VMEM((slots, GROUPS, 2 * ROWS, WIDE), BF16),
            pltpu.VMEM((GROUPS, 2 * ROWS, WIDE), F32),
            pltpu.VMEM((slots, WIDE), F32),
            pltpu.VMEM((slots, GROUPS * WIDE), F32),
            pltpu.VMEM((slots, ROWS, WIDE), F32),
            pltpu.VMEM((slots, WIDE), F32),
            pltpu.VMEM((slots, ROWS, 128), F32),
            pltpu.VMEM((GROUPS, 2 * ROWS, WIDE), BF16),
            pltpu.SemaphoreType.DMA((count,)),
            pltpu.SemaphoreType.DMA((count,)),
        ],
        compiler_params=pltpu.CompilerParams(
            vmem_limit_bytes=48 * 2**20, collective_id=0, has_side_effects=True
        ),
    )(
        slot_ref,
        tri_count,
        packed[:sent].reshape(count, cap, ROWS, 128),
        packed[sent : sent + slots],
        packed[sent + slots :],
        force,
        freqs[sent : sent + slots],
        freqs[sent + slots :],
        local_q[:, None],
        slot_ref[None, :],
        *[jnp.asarray(held[name]) for name in NAMES],
    )
    return pl.pallas_call(
        functools.partial(finish_kernel, count),
        out_shape=jax.ShapeDtypeStruct((NB, owned), F32),
        in_specs=[vmem] * 3,
        out_specs=vmem,
        scratch_shapes=[
            pltpu.VMEM((count, cap, NB), F32),
            pltpu.SemaphoreType.DMA((count,)),
            pltpu.SemaphoreType.DMA((count,)),
        ],
        compiler_params=pltpu.CompilerParams(collective_id=1, has_side_effects=True),
    )(rates, by_slot, outgoing[:, None])


def solution(mesh):
    split = P(("groups", "pb"))
    rows = P(("groups", "pb"), None)
    return jax.shard_map(
        on_device,
        mesh=mesh,
        in_specs=(rows, rows, P(), rows, split, split, split, split),
        out_specs=P(None, ("groups", "pb")),
        check_vma=False,
    )
```
